256 devices in a mesh: col: 8 (over z), leaf: 32 (over y, x, core).
Axes of the slice: x: 4, y: 4, z: 8, core: 2. Of those that a mesh axis runs over, the one named last changes fastest.
Arguments:
- voltage: bfloat16 [128, 128, 4, 2048], P(None, 'leaf', None, 'col'), may hold values from -4 to 4
- source: bfloat16 [128, 128, 4, 2048], P(None, 'leaf', None, 'col'), may hold values from -6 to 6
- conduct: float32 [128, 4, 2048], P('leaf', None, 'col'), may hold values from 0.25 to 2
- leaf_inverse: bfloat16 [128, 4, 2048, 256], P('leaf', None, 'col'), as said below
- update_rows: int32 [8, 128, 4, 2], P('col', 'leaf'), may hold values from 0 to 127, as said below
- update_matrix: bfloat16 [128, 4, 256, 2048], P('leaf', None, None, 'col'), may hold values from -0.1875 to 0.1875
- chain_slot: int32 [64], replicated, may hold values from 0 to 63, as said below
- separator_source: float32 [128, 64, 2048], P(None, 'leaf', 'col'), may hold values from -6 to 6
- separator_inverse: float32 [64, 2048, 256], P('leaf', 'col'), as said below
- separator_coupling: float32 [64, 2048, 256], P('leaf', 'col'), may hold values from -0.3125 to 0.3125
Outputs:
- leaf_result: float32 [128, 128, 4, 2048], P(None, 'leaf', None, 'col')
- separator_result: float32 [128, 64, 2048], P(None, 'leaf', 'col')
The draws below stay inside these ranges and needn't reach their ends.
Inputs may be any that keep to these rules, and one draw needn't show every extreme that they name: `update_rows`: row [q, x, y] names 2 different update-row blocks of the separator panels at position q; block t holds rows (t % 2) * 128 onward of chain t // 2. Among the 32 entries of the rows [q, x, y] held by one device, at most 2 name blocks whose chains are stored in storage rows i * 2 to (i + 1) * 2 - 1 for one i, and exactly 2 do for some i on every device. A permutation: chain j is stored at row chain_slot[j] of the separator arrays. `leaf_inverse`: each 256 x 256 block is a given inverse of a diagonal block. `separator_inverse`: each 256 x 256 block is a given inverse of a diagonal block.
All inputs are finite; a program needn't handle non-finite values.
Results may differ from the reference program's by a relative error of at most 0.0039.
Values may be sent and summed in bfloat16 or wider, within the bound.
No kernel may reach another device: no remote copies, remote signals or barrier semaphores. Data moves between devices by JAX's collectives and lax.ppermute only.
A program may use at most 128 MiB of HBM per device.

```python
import math
import jax
import jax.numpy as jnp
from jax import lax

NRHS = 128
CX = 4
CY = 4
PANEL = 256
BLK = 128
K = 2
SEP_DEV = 2
NX = 128
NY = 4
NZ = 2048
SCHAIN = 64
NSEP = 2048
CAP = 2
N_COL = 8


def inverse_blocks(key, shape):
    rows = lax.broadcasted_iota(jnp.int32, shape, len(shape) - 2) % PANEL
    cols = lax.broadcasted_iota(jnp.int32, shape, len(shape) - 1)
    first_key, second_key = jax.random.split(key)
    diag_part = jnp.exp(jax.random.uniform(first_key, shape, jnp.float32, math.log(0.5), math.log(2.0)))
    off_part = jax.random.normal(second_key, shape, jnp.float32) * (0.5 / math.sqrt(PANEL))
    return jnp.where(rows == cols, diag_part, off_part)


def draw_leaf_inverse(key, part):
    return inverse_blocks(jax.random.fold_in(key, 11), (NX, NY, NZ, PANEL)).astype(jnp.bfloat16)


def draw_separator_inverse(key, part):
    return inverse_blocks(jax.random.fold_in(key, 23), (SCHAIN, NSEP, PANEL)).astype(jnp.float32)


def routing_tables(key):
    base = jax.random.fold_in(key, 77)
    order_key, owner_key, offset_key = jax.random.split(base, 3)
    leaves = NX // CX
    columns = NZ // PANEL
    halves = PANEL // BLK
    local_targets = SEP_DEV * halves
    order_score = jax.random.randint(order_key, (SCHAIN,), 0, 1 << 20, jnp.int32) * SCHAIN + jnp.arange(SCHAIN, dtype=jnp.int32)
    chain_of_slot = jnp.argsort(order_score, stable=True).astype(jnp.int32)
    slot_of_chain = jnp.argsort(chain_of_slot, stable=True).astype(jnp.int32)
    owner_score = jax.random.randint(owner_key, (columns, leaves, leaves), 0, 1 << 20, jnp.int32) * leaves + lax.broadcasted_iota(jnp.int32, (columns, leaves, leaves), 2)
    owner_order = jnp.argsort(owner_score, axis=2, stable=True).astype(jnp.int32)
    offsets = jax.random.randint(offset_key, (columns, leaves, leaves), 0, local_targets, jnp.int32)
    entry = jnp.arange(CX * CY * K, dtype=jnp.int32)
    group = entry // CAP
    within = entry % CAP
    owner = owner_order[:, :, group]
    local = (offsets[:, :, group] + within) % local_targets
    slot = owner * SEP_DEV + local // halves
    targets = chain_of_slot[slot] * halves + local % halves
    rows = targets.reshape(columns, leaves * CX, CY, K).astype(jnp.int32)
    return (rows, slot_of_chain)


def draw_update_rows(key, part):
    rows, slot_of_chain = routing_tables(key)
    return rows


def draw_chain_slot(key, part):
    rows, slot_of_chain = routing_tables(key)
    return slot_of_chain


def levels(rng, shape, pieces, low, largest):
    def one(axis_at, shards_of):
        draws = jax.random.uniform(jax.random.fold_in(jax.random.fold_in(rng, 6), axis_at), (shards_of,), jnp.float32, low / len(pieces), largest / len(pieces))
        return jnp.repeat(jnp.exp(draws), shape[axis_at] // shards_of).reshape((-1,) + (1,) * (len(shape) - axis_at - 1))

    gain = one(*pieces[0])
    for cut in pieces[1:]:
        gain = gain * one(*cut)
    return gain


def gaussian(stream_key, extent, deviation, limit, shards=(), kind=jnp.bfloat16):
    drawn = deviation * jax.random.normal(stream_key, extent, jnp.float32)
    if shards:
        drawn = drawn * levels(stream_key, extent, shards, -0.22, 0.18)
    return jnp.clip(drawn, -limit, limit).astype(kind)


def setup_inputs(seed: int = 0) -> dict:
    arg_keys = jax.random.split(jax.random.key(seed), 11)
    voltage = gaussian(arg_keys[0], (NRHS, NX, NY, NZ), 0.3, 4.0, ((1, 32), (3, 8)))
    source = gaussian(arg_keys[1], (NRHS, NX, NY, NZ), 1.0, 6.0, ((1, 32), (3, 8)))
    conduct = jnp.clip(0.25 + 1.75 * jax.random.uniform(arg_keys[2], (NX, NY, NZ), jnp.float32) ** levels(arg_keys[2], (NX, NY, NZ), ((0, 32), (2, 8)), -0.2, 0.2), 0.25, 2.0)
    leaf_inverse = draw_leaf_inverse(jax.random.fold_in(arg_keys[10], 71), 0)
    update_rows = draw_update_rows(jax.random.fold_in(arg_keys[10], 71), 0)
    update_matrix = gaussian(arg_keys[5], (NX, NY, K * BLK, NZ), (4 * PANEL) ** -0.5, 0.1875, ((0, 32), (3, 8)))
    chain_slot = draw_chain_slot(jax.random.fold_in(arg_keys[10], 71), 0)
    separator_source = gaussian(arg_keys[7], (NRHS, SCHAIN, NSEP), 1.0, 6.0, ((1, 32), (2, 8)), jnp.float32)
    separator_inverse = draw_separator_inverse(jax.random.fold_in(arg_keys[10], 71), 0)
    separator_coupling = gaussian(arg_keys[9], (SCHAIN, NSEP, PANEL), (PANEL * 3 // 2) ** -0.5, 0.3125, ((0, 32), (1, 8)), jnp.float32)
    return dict(voltage=voltage, source=source, conduct=conduct, leaf_inverse=leaf_inverse, update_rows=update_rows, update_matrix=update_matrix, chain_slot=chain_slot, separator_source=separator_source, separator_inverse=separator_inverse, separator_coupling=separator_coupling)


def reference(voltage, source, conduct, leaf_inverse, update_rows, update_matrix, chain_slot, separator_source, separator_inverse, separator_coupling):
    highest = lax.Precision.HIGHEST
    fields = voltage.shape[0]
    halves = PANEL // BLK
    volt_wide = voltage.astype(jnp.float32)
    padded = jnp.pad(volt_wide, ((0, 0), (1, 1), (1, 1), (1, 1)))
    beside = padded[:, 2:, 1:-1, 1:-1] + padded[:, :-2, 1:-1, 1:-1]
    beside = beside + padded[:, 1:-1, 2:, 1:-1] + padded[:, 1:-1, :-2, 1:-1]
    beside = beside + padded[:, 1:-1, 1:-1, 2:] + padded[:, 1:-1, 1:-1, :-2]
    residual = source.astype(jnp.float32) - ((6.0 + conduct) * volt_wide - beside)
    residual_low = residual.astype(jnp.bfloat16).reshape(fields, NX, NY, N_COL, PANEL)
    target_slot = chain_slot[update_rows // halves].astype(jnp.int32)
    target_half = update_rows % halves
    slot_x = jnp.moveaxis(target_slot, 1, 0)
    half_x = jnp.moveaxis(target_half, 1, 0)
    inverse_x = leaf_inverse.reshape(NX, NY, N_COL, PANEL, PANEL)
    matrix_x = update_matrix.reshape(NX, NY, K, BLK, N_COL, PANEL)
    residual_x = jnp.moveaxis(residual_low, 1, 0)

    def make_picker(slots, halfs):
        slot_hit = (slots[..., None] == jnp.arange(SCHAIN, dtype=jnp.int32)).astype(jnp.float32)
        half_hit = (halfs[..., None] == jnp.arange(halves, dtype=jnp.int32)).astype(jnp.float32)
        return slot_hit[..., :, None] * half_hit[..., None, :]

    def forward_step(dense, slices):
        resid_now, inverse_now, matrix_now, slots, halfs = slices
        resid_wide = resid_now.astype(jnp.float32)
        scaled = jnp.einsum("yqab,nyqb->nyqa", inverse_now.astype(jnp.float32), resid_wide, precision=highest)
        contrib = jnp.einsum("ykjqb,nyqb->qyknj", matrix_now.astype(jnp.float32), resid_wide, precision=highest)
        picker = make_picker(slots, halfs)
        dense = dense + jnp.einsum("qyksh,qyknj->nsqhj", picker, contrib, precision=highest)
        return dense, scaled

    dense_init = jnp.zeros((fields, SCHAIN, N_COL, halves, BLK), jnp.float32)
    dense, leaf_scaled = lax.scan(forward_step, dense_init, (residual_x, inverse_x, matrix_x, slot_x, half_x))
    drive = separator_source.reshape(fields, SCHAIN, N_COL, PANEL) - dense.reshape(fields, SCHAIN, N_COL, PANEL)
    coupling = separator_coupling.reshape(SCHAIN, N_COL, PANEL, PANEL)
    sep_inverse = separator_inverse.reshape(SCHAIN, N_COL, PANEL, PANEL)
    forward_values = []
    previous = None
    for column in range(N_COL):
        current = drive[:, :, column]
        if column > 0:
            current = current - jnp.einsum("eab,neb->nea", coupling[:, column], previous, precision=highest)
        forward_values.append(current)
        previous = current
    scaled_sep = [jnp.einsum("eab,neb->nea", sep_inverse[:, column], forward_values[column], precision=highest) for column in range(N_COL)]
    results = [None] * N_COL
    following = None
    for column in reversed(range(N_COL)):
        current = scaled_sep[column]
        if column < N_COL - 1:
            current = current - jnp.einsum("eba,neb->nea", coupling[:, column + 1], following, precision=highest)
        results[column] = current
        following = current
    separator_result = jnp.stack(results, axis=2).reshape(fields, SCHAIN, NSEP)
    separator_low = separator_result.astype(jnp.bfloat16).reshape(fields, SCHAIN, N_COL, halves, BLK).astype(jnp.float32)

    def backward_step(slices):
        scaled_now, matrix_now, slots, halfs = slices
        picker = make_picker(slots, halfs)
        picked = jnp.einsum("qyksh,nsqhj->qyknj", picker, separator_low, precision=highest)
        correction = jnp.einsum("ykjqb,qyknj->nyqb", matrix_now.astype(jnp.float32), picked, precision=highest)
        return scaled_now - correction

    leaf_out = lax.map(backward_step, (leaf_scaled, matrix_x, slot_x, half_x))
    leaf_result = jnp.moveaxis(leaf_out, 0, 1).reshape(fields, NX, NY, NZ)
    return leaf_result, separator_result
```

```python
import functools
import jax
import jax.numpy as jnp
from jax import lax
from jax.experimental import pallas as pl
from jax.experimental.pallas import tpu as pltpu
from jax.sharding import PartitionSpec as P

VM = pl.BlockSpec(memory_space=pltpu.VMEM)
HB = pl.BlockSpec(memory_space=pltpu.HBM)
SM = pl.BlockSpec(memory_space=pltpu.SMEM)
F32 = jnp.float32
BF16 = jnp.bfloat16
MIB = 1 << 20
FACTOR_MIB = 56


def dot(a, b, kind):
    dims = {"nt": (((1,), (1,)), ((), ())), "nn": (((1,), (0,)), ((), ()))}[kind]
    return lax.dot_general(a, b, dims, preferred_element_type=F32)


def split(x):
    high = x.astype(BF16)
    return high, (x - high.astype(F32)).astype(BF16)


def dot3(a, b, kind):
    high, low = split(a)
    b_high, b_low = split(b)
    axis = 1 if kind == "nt" else 0
    left = jnp.concatenate([high, low, high], axis=1)
    right = jnp.concatenate([b_high, b_high, b_low], axis=axis)
    return dot(left, right, kind)


def leaf_kernel(extent_y, slot, volt, source, diag, below, above, left, right, blocks, marks, low_out, sent):
    panels, fields, width = volt.shape
    rows = sent.shape[2]
    per_leaf = slot.shape[0] // panels
    capacity = sent.shape[1] // fields
    sent[:, : capacity * fields, :] = jnp.zeros((sent.shape[0], capacity * fields, rows), BF16)
    sent[:, capacity * fields :, :] = marks[...]
    lane = lax.broadcasted_iota(jnp.int32, (fields, width), 1)
    rest = jnp.zeros((fields - 2 * panels, left.shape[1]), F32)
    sides = jnp.transpose(jnp.concatenate([left[...], right[...], rest], axis=0))
    for p in range(panels):
        y = p % extent_y
        center = volt[p].astype(F32)
        x_low = below[y] if p < extent_y else volt[p - extent_y]
        x_high = above[y] if p >= panels - extent_y else volt[p + extent_y]
        beside = x_high.astype(F32) + x_low.astype(F32)
        z_low = jnp.where(lane == 0, sides[:, p : p + 1], pltpu.roll(center, 1, 1))
        z_high = jnp.where(lane == width - 1, sides[:, panels + p : panels + p + 1], pltpu.roll(center, width - 1, 1))
        beside = beside + z_high + z_low
        if y + 1 < extent_y:
            beside = beside + volt[p + 1].astype(F32)
        if y > 0:
            beside = beside + volt[p - 1].astype(F32)
        residual = source[p].astype(F32) - (diag[p : p + 1, :] * center - beside)
        low = residual.astype(BF16)
        low_out[p] = low
        product = dot(low, blocks[p], "nt").astype(BF16)
        for k in range(per_leaf):
            s = slot[p * per_leaf + k]
            start = pl.multiple_of(lax.rem(s, capacity) * fields, fields)
            sent[lax.div(s, capacity), pl.ds(start, fields), :] = product[:, k * rows : (k + 1) * rows]


def scaled_kernel(low, inverse, out):
    for p in range(low.shape[0]):
        out[p] = dot(low[p], inverse[p], "nt")


def owner_kernel(capacity, received, own, drive, tags):
    sep_rows, fields, width = own.shape
    owners, _, rows = received.shape
    halves = width // rows
    count = sep_rows * halves
    step = 32

    def mark(s, r):
        return received[s, capacity * fields : capacity * fields + 16, :].astype(F32)[8 * r : 8 * r + 8]

    lane = lax.broadcasted_iota(jnp.int32, (1, rows), 1)
    for s in range(owners):
        line = mark(s, 0)[:1]
        for r in range(1, capacity):
            line = jnp.where(lane == r, mark(s, r)[:1], line)
        tags[s : s + 1, :] = line
    for c in range(fields // step):
        span = slice(c * step, (c + 1) * step)
        first = []
        for b in range(count):
            first.append(own[b // halves, span, (b % halves) * rows : (b % halves + 1) * rows])

        def add(s, totals):
            totals = list(totals)
            for r in range(capacity):
                tag = jnp.concatenate([mark(s, r)] * (step // 8), axis=0)
                start = r * fields + c * step
                block = received[s, start : start + step, :].astype(F32)
                for b in range(count):
                    totals[b] = totals[b] - jnp.where(tag == float(b), block, 0.0)
            return tuple(totals)

        totals = lax.fori_loop(0, owners, add, tuple(first), unroll=4)
        for b in range(count):
            drive[b // halves, span, (b % halves) * rows : (b % halves + 1) * rows] = totals[b].astype(BF16)


def pack_kernel(coupling, inverse, last_z, first_z, out):
    width = coupling.shape[2]
    for e in range(coupling.shape[0]):
        block = inverse[e]
        biggest = jnp.max(jnp.max(jnp.abs(block), axis=1, keepdims=True), axis=0, keepdims=True)
        power = jnp.clip(jnp.ceil(jnp.log2(biggest)), -120.0, 120.0)
        out[e, :width, :] = coupling[e]
        out[e, width : 2 * width, :] = block * jnp.exp2(-power)
        out[e, 2 * width : 2 * width + 8, :] = jnp.broadcast_to(power, (8, width))
        out[e, 2 * width + 8 :, :] = jnp.concatenate([last_z[...], first_z[...]], axis=1).astype(F32)


def factor_kernel(columns, place, *refs):
    pieces, (m_high, m_low, ring, z, y, sems) = refs[:columns], refs[columns:]
    chains, _, width = pieces[0].shape
    copies = [pltpu.make_async_copy(pieces[k], ring.at[k], sems.at[k]) for k in range(columns)]
    for copy in copies:
        copy.start()
    q = place[0]

    def at(p):
        return lax.rem(p - q + columns, columns)

    def coupling(rel, e):
        return ring[rel, e, :width, :]

    def inverse(rel, e):
        return ring[rel, e, width : 2 * width, :] * jnp.exp2(ring[rel, e, 2 * width : 2 * width + 1, :])

    row = lax.broadcasted_iota(jnp.int32, (width, width), 0)
    col = lax.broadcasted_iota(jnp.int32, (width, width), 1)
    eye = (row == col).astype(F32)
    copies[0].wait()
    for e in range(chains):
        z[q, e] = inverse(0, e)
        y[e] = eye
    for k in range(1, columns):
        copies[k].wait()

        @pl.when(q + k < columns)
        def _(k=k):
            out = [-dot3(y[e], coupling(k, e), "nt") for e in range(chains)]
            for e in range(chains):
                y[e] = out[e]
                z[q + k, e] = dot3(out[e], inverse(k, e), "nn")

    def put(p, xs):
        rel = at(p)
        for e in range(chains):
            high, low = split(xs[e])
            m_high[rel, e] = high
            m_low[rel, e] = low

    last = tuple(z[columns - 1, e] for e in range(chains))
    put(columns - 1, last)

    def up(i, xs):
        p = columns - 2 - i
        rel = at(p + 1)
        out = []
        for e in range(chains):
            x = -dot3(xs[e], coupling(rel, e), "nn")
            out.append(x + jnp.where(p >= q, z[p, e], 0.0))
        put(p, out)
        return tuple(out)

    lax.fori_loop(0, columns - 1, up, last)


def solve_kernel(columns, tag, m_high, m_low, *refs):
    drives, (result, sent, low) = refs[:columns], refs[columns:]
    sep_rows, fields, width = result.shape
    rows = sent.shape[2]
    halves = width // rows
    for e in range(sep_rows):
        acc = jnp.zeros((fields, width), F32)
        for k in range(columns):
            d = drives[k][e]
            acc = acc + dot(d, m_high[k, e], "nt") + dot(d, m_low[k, e], "nt")
        result[e] = acc
        narrow = acc.astype(BF16)
        for h in range(halves):
            low[e * halves + h] = narrow[:, h * rows : (h + 1) * rows]

    def pick(s, carry):
        sent[s] = low[jnp.maximum(tag[s], 0)]
        return carry

    lax.fori_loop(0, sent.shape[0], pick, 0, unroll=4)


def finish_kernel(extent_y, slot, scaled, blocks, received, out):
    panels, fields, width = scaled.shape
    lanes = width // 128
    group = out.shape[0] // fields
    per_leaf = slot.shape[0] // panels
    for p in range(panels):
        picked = [received[slot[p * per_leaf + k]] for k in range(per_leaf)]
        acc = scaled[p] - dot(jnp.concatenate(picked, axis=1), blocks[p], "nn")
        x, y = divmod(p, extent_y)
        for part in range(lanes):
            start = (x * lanes + part) * extent_y + y
            out[pl.ds(start, fields, stride=group), :] = acc[:, part * 128 : (part + 1) * 128]


def call(kernel, out_shape, in_specs, out_specs, limit, scratch=(), flops=0, moved=0):
    return pl.pallas_call(
        kernel,
        out_shape=out_shape,
        in_specs=in_specs,
        out_specs=out_specs,
        scratch_shapes=list(scratch),
        compiler_params=pltpu.CompilerParams(vmem_limit_bytes=limit * MIB),
        cost_estimate=pl.CostEstimate(flops=flops, bytes_accessed=moved, transcendentals=0),
    )


def level(
    voltage,
    source,
    conduct,
    leaf_inverse,
    update_rows,
    update_matrix,
    chain_slot,
    separator_source,
    separator_inverse,
    separator_coupling,
):
    fields, extent_x, extent_y, width = voltage.shape
    per_leaf = update_rows.shape[3]
    rows = update_matrix.shape[2] // per_leaf
    halves = width // rows
    panels = extent_x * extent_y
    chains = chain_slot.shape[0]
    sep_rows = separator_source.shape[1]
    owners = lax.axis_size("leaf")
    columns = lax.axis_size("col")
    entries = panels * per_leaf
    capacity = 2
    slots = owners * capacity
    shape = jax.ShapeDtypeStruct

    def shifted(block, axis, distance, wrap=False):
        size = lax.axis_size(axis)
        route = [(i, (i + distance) % size) for i in range(size) if wrap or 0 <= i + distance < size]
        return lax.ppermute(block, axis, route)

    fresh = lax.optimization_barrier(voltage)
    padded = call(
        pack_kernel,
        shape((sep_rows, 2 * width + 8 + panels, width), F32),
        [VM] * 4,
        VM,
        8,
        moved=2 << 20,
    )(
        separator_coupling,
        separator_inverse,
        jnp.transpose(fresh[:, :, :, width - 1].reshape(fields, panels)),
        jnp.transpose(fresh[:, :, :, 0].reshape(fields, panels)),
    )
    edges = (
        jnp.transpose(fresh[:, extent_x - 1], (1, 0, 2)),
        jnp.transpose(fresh[:, 0], (1, 0, 2)),
        padded.astype(jnp.float16),
    )
    last_x, first_x, packed = lax.optimization_barrier(edges)
    below = shifted(last_x, "leaf", 1)
    above = shifted(first_x, "leaf", -1)

    targets = update_rows.reshape(entries)
    chain_hit = (targets // halves)[:, None] == jnp.arange(chains, dtype=jnp.int32)
    target_slot = jnp.sum(jnp.where(chain_hit, chain_slot, 0), axis=1)
    owner = target_slot // sep_rows
    local = target_slot % sep_rows * halves + targets % halves
    ids = jnp.arange(entries, dtype=jnp.int32)
    same = (owner[:, None] == owner[None, :]) & (ids[None, :] < ids[:, None])
    slot = owner * capacity + jnp.sum(same.astype(jnp.int32), axis=1)
    slot_hit = slot[:, None] == jnp.arange(slots, dtype=jnp.int32)[None, :]
    out_tags = jnp.sum(jnp.where(slot_hit, local[:, None] + 1, 0), axis=0) - 1
    marks = jnp.broadcast_to(out_tags.astype(BF16).reshape(owners, capacity, 1, 1), (owners, capacity, 8, rows))
    marks = marks.reshape(owners, capacity * 8, rows)

    pieces = [padded] + [None] * (columns - 1)
    up = down = packed
    for hop in range(1, columns // 2):
        up = shifted(up, "col", 1, True)
        down = shifted(down, "col", -1, True)
        pieces[columns - hop] = up
        pieces[hop] = down
    column = lax.axis_index("col")
    left = pieces[columns - 1][0, 2 * width + 8 :, :fields].astype(F32)
    left = jnp.where(column > 0, left, 0.0)
    right = pieces[1][0, 2 * width + 8 :, fields : 2 * fields].astype(F32)
    right = jnp.where(column < columns - 1, right, 0.0)
    middle = sep_rows // 2
    up = shifted(up[:middle], "col", 1, True)
    down = shifted(down[middle:], "col", -1, True)
    for k in range(1, columns):
        if k != columns // 2:
            pieces[k] = pieces[k].astype(F32)
    pieces[columns // 2] = jnp.concatenate([up.astype(F32), down.astype(F32)], axis=0)

    blocks = update_matrix.reshape(panels, per_leaf * rows, width)
    inverse = leaf_inverse.reshape(panels, width, width)
    p_major = (1, 0, 2)
    low, sent = call(
        functools.partial(leaf_kernel, extent_y),
        (shape((panels, fields, width), BF16), shape((owners, capacity * fields + 16, rows), BF16)),
        [SM] + [VM] * 9,
        (VM, VM),
        12,
        flops=2 * panels * fields * width * width,
        moved=8 << 20,
    )(
        slot,
        jnp.transpose(voltage.reshape(fields, panels, width), p_major),
        jnp.transpose(source.reshape(fields, panels, width), p_major),
        (6.0 + conduct).reshape(panels, width),
        below,
        above,
        left,
        right,
        blocks,
        marks,
    )

    scaled = call(
        scaled_kernel,
        shape((panels, fields, width), F32),
        [VM, VM],
        VM,
        8,
        flops=2 * panels * fields * width * width,
        moved=6 << 20,
    )(low, inverse)

    def exchange(block):
        return lax.all_to_all(block, "leaf", split_axis=0, concat_axis=0, tiled=True)

    arrived = exchange(sent)
    drive, tags = call(
        functools.partial(owner_kernel, capacity),
        (shape((sep_rows, fields, width), BF16), shape((owners, rows), F32)),
        [VM, VM],
        (VM, VM),
        6,
        flops=slots * fields * rows,
        moved=3 << 20,
    )(arrived, jnp.transpose(separator_source, p_major))
    in_tags = tags[:, :capacity].reshape(slots).astype(jnp.int32)

    place = column.astype(jnp.int32).reshape(1)
    square = shape((columns, sep_rows, width, width), BF16)
    m_high, m_low = call(
        functools.partial(factor_kernel, columns),
        (square, square),
        [SM] + [HB] * columns,
        (VM, VM),
        FACTOR_MIB,
        scratch=[
            pltpu.VMEM((columns,) + packed.shape, F32),
            pltpu.VMEM((columns, sep_rows, width, width), F32),
            pltpu.VMEM((sep_rows, width, width), F32),
            pltpu.SemaphoreType.DMA((columns,)),
        ],
        flops=2 * 126 * width**3,
        moved=12 << 20,
    )(place, *pieces)

    drives = [drive] + [shifted(drive, "col", -k, True) for k in range(1, columns)]
    result, answer = call(
        functools.partial(solve_kernel, columns),
        (shape((sep_rows, fields, width), F32), shape((slots, fields, rows), BF16)),
        [SM] + [VM] * (2 + columns),
        (VM, VM),
        10,
        scratch=[pltpu.VMEM((sep_rows * halves, fields, rows), BF16)],
        flops=4 * columns * sep_rows * fields * width * width,
        moved=8 << 20,
    )(in_tags, m_high, m_low, *drives)
    returned = exchange(answer.reshape(owners, capacity, fields, rows)).reshape(slots, fields, rows)
    flat = call(
        functools.partial(finish_kernel, extent_y),
        shape((fields * panels * width // 128, 128), F32),
        [SM] + [VM] * 3,
        VM,
        12,
        flops=2 * panels * fields * width * width,
        moved=8 << 20,
    )(slot, scaled, blocks, returned)
    lanes = width // 128
    leaf_result = flat.reshape(fields, extent_x, lanes, extent_y, 128)
    leaf_result = jnp.transpose(leaf_result, (0, 1, 3, 2, 4)).reshape(voltage.shape)
    return leaf_result, jnp.transpose(result, p_major)


def solution(mesh):
    placed = (
        P(None, "leaf", None, "col"),
        P(None, "leaf", None, "col"),
        P("leaf", None, "col"),
        P("leaf", None, "col", None),
        P("col", "leaf", None, None),
        P("leaf", None, None, "col"),
        P(),
        P(None, "leaf", "col"),
        P("leaf", "col", None),
        P("leaf", "col", None),
    )
    return jax.shard_map(
        level,
        mesh=mesh,
        in_specs=placed,
        out_specs=(P(None, "leaf", None, "col"), P(None, "leaf", "col")),
        check_vma=False,
    )
```

```python
import functools
import jax
import jax.numpy as jnp
from jax import lax
from jax.experimental import pallas as pl
from jax.experimental.pallas import tpu as pltpu
from jax.sharding import PartitionSpec as P

VM = pl.BlockSpec(memory_space=pltpu.VMEM)
HB = pl.BlockSpec(memory_space=pltpu.HBM)
SM = pl.BlockSpec(memory_space=pltpu.SMEM)
F32 = jnp.float32
BF16 = jnp.bfloat16
MIB = 1 << 20
FACTOR_MIB = 24


def dot(a, b, kind):
    dims = {"nt": (((1,), (1,)), ((), ())), "nn": (((1,), (0,)), ((), ()))}[kind]
    return lax.dot_general(a, b, dims, preferred_element_type=F32)


def split(x):
    high = x.astype(BF16)
    return high, (x - high.astype(F32)).astype(BF16)


def dot3(a, b, kind):
    high, low = split(a)
    b_high, b_low = split(b)
    axis = 1 if kind == "nt" else 0
    left = jnp.concatenate([high, low, high], axis=1)
    right = jnp.concatenate([b_high, b_high, b_low], axis=axis)
    return dot(left, right, kind)


def leaf_kernel(extent_y, slot, volt, source, diag, below, above, left, right, blocks, marks, low_out, sent):
    panels, fields, width = volt.shape
    rows = sent.shape[2]
    per_leaf = slot.shape[0] // panels
    capacity = sent.shape[1] // fields
    sent[:, : capacity * fields, :] = jnp.zeros((sent.shape[0], capacity * fields, rows), BF16)
    sent[:, capacity * fields :, :] = marks[...]
    lane = lax.broadcasted_iota(jnp.int32, (fields, width), 1)
    rest = jnp.zeros((fields - 2 * panels, left.shape[1]), F32)
    sides = jnp.transpose(jnp.concatenate([left[...], right[...], rest], axis=0))
    for p in range(panels):
        y = p % extent_y
        center = volt[p].astype(F32)
        x_low = below[y] if p < extent_y else volt[p - extent_y]
        x_high = above[y] if p >= panels - extent_y else volt[p + extent_y]
        beside = x_high.astype(F32) + x_low.astype(F32)
        z_low = jnp.where(lane == 0, sides[:, p : p + 1], pltpu.roll(center, 1, 1))
        z_high = jnp.where(lane == width - 1, sides[:, panels + p : panels + p + 1], pltpu.roll(center, width - 1, 1))
        beside = beside + z_high + z_low
        if y + 1 < extent_y:
            beside = beside + volt[p + 1].astype(F32)
        if y > 0:
            beside = beside + volt[p - 1].astype(F32)
        residual = source[p].astype(F32) - (diag[p : p + 1, :] * center - beside)
        low = residual.astype(BF16)
        low_out[p] = low
        product = dot(low, blocks[p], "nt").astype(BF16)
        for k in range(per_leaf):
            s = slot[p * per_leaf + k]
            start = pl.multiple_of(lax.rem(s, capacity) * fields, fields)
            sent[lax.div(s, capacity), pl.ds(start, fields), :] = product[:, k * rows : (k + 1) * rows]


def scaled_kernel(low, inverse, out):
    for p in range(low.shape[0]):
        out[p] = dot(low[p], inverse[p], "nt")


def owner_kernel(capacity, received, own, drive, tags):
    sep_rows, fields, width = own.shape
    owners, _, rows = received.shape
    halves = width // rows
    count = sep_rows * halves
    step = 32

    def mark(s, r):
        return received[s, capacity * fields : capacity * fields + 8, :].astype(F32)[r : r + 1]

    lane = lax.broadcasted_iota(jnp.int32, (1, rows), 1)
    for s in range(owners):
        line = mark(s, 0)
        for r in range(1, capacity):
            line = jnp.where(lane == r, mark(s, r), line)
        tags[s : s + 1, :] = line
    for c in range(fields // step):
        span = slice(c * step, (c + 1) * step)
        first = []
        for b in range(count):
            first.append(own[b // halves, span, (b % halves) * rows : (b % halves + 1) * rows])

        def add(s, totals):
            totals = list(totals)
            for r in range(capacity):
                tag = jnp.broadcast_to(mark(s, r), (step, rows))
                start = r * fields + c * step
                block = received[s, start : start + step, :].astype(F32)
                for b in range(count):
                    totals[b] = totals[b] - jnp.where(tag == float(b), block, 0.0)
            return tuple(totals)

        totals = lax.fori_loop(0, owners, add, tuple(first), unroll=4)
        for b in range(count):
            drive[b // halves, span, (b % halves) * rows : (b % halves + 1) * rows] = totals[b].astype(BF16)


def pack_kernel(coupling, inverse, last_z, first_z, out):
    width = coupling.shape[2]
    for e in range(coupling.shape[0]):
        block = inverse[e]
        biggest = jnp.max(jnp.max(jnp.abs(block), axis=1, keepdims=True), axis=0, keepdims=True)
        power = jnp.clip(jnp.ceil(jnp.log2(biggest)), -120.0, 120.0)
        out[e, :width, :] = coupling[e]
        out[e, width : 2 * width, :] = block * jnp.exp2(-power)
        out[e, 2 * width : 2 * width + 8, :] = jnp.broadcast_to(power, (8, width))
        out[e, 2 * width + 8 :, :] = jnp.concatenate([last_z[...], first_z[...]], axis=1).astype(F32)


def factor_kernel(columns, place, *refs):
    pieces, (m_high, m_low, ring, z, y, sems) = refs[:columns], refs[columns:]
    chains, _, width = pieces[0].shape
    copies = [pltpu.make_async_copy(pieces[k], ring.at[k], sems.at[k]) for k in range(columns)]
    for copy in copies:
        copy.start()
    q = place[0]

    def at(p):
        return lax.rem(p - q + columns, columns)

    def coupling(rel, e):
        return ring[rel, e, :width, :]

    def inverse(rel, e):
        return ring[rel, e, width : 2 * width, :] * jnp.exp2(ring[rel, e, 2 * width : 2 * width + 1, :])

    row = lax.broadcasted_iota(jnp.int32, (width, width), 0)
    col = lax.broadcasted_iota(jnp.int32, (width, width), 1)
    eye = (row == col).astype(F32)
    copies[0].wait()
    for e in range(chains):
        z[q, e] = inverse(0, e)
        y[e] = eye
    for k in range(1, columns):
        copies[k].wait()

        @pl.when(q + k < columns)
        def _(k=k):
            out = [-dot3(y[e], coupling(k, e), "nt") for e in range(chains)]
            for e in range(chains):
                y[e] = out[e]
                z[q + k, e] = dot3(out[e], inverse(k, e), "nn")

    def put(p, xs):
        rel = at(p)
        for e in range(chains):
            high, low = split(xs[e])
            m_high[rel, e] = high
            m_low[rel, e] = low

    last = tuple(z[columns - 1, e] for e in range(chains))
    put(columns - 1, last)

    def up(i, xs):
        p = columns - 2 - i
        rel = at(p + 1)
        out = []
        for e in range(chains):
            x = -dot3(xs[e], coupling(rel, e), "nn")
            out.append(x + jnp.where(p >= q, z[p, e], 0.0))
        put(p, out)
        return tuple(out)

    lax.fori_loop(0, columns - 1, up, last)


def solve_kernel(columns, tag, m_high, m_low, *refs):
    drives, (result, sent, low) = refs[:columns], refs[columns:]
    sep_rows, fields, width = result.shape
    rows = sent.shape[2]
    halves = width // rows
    for e in range(sep_rows):
        acc = jnp.zeros((fields, width), F32)
        for k in range(columns):
            d = drives[k][e]
            acc = acc + dot(d, m_high[k, e], "nt") + dot(d, m_low[k, e], "nt")
        result[e] = acc
        narrow = acc.astype(BF16)
        for h in range(halves):
            low[e * halves + h] = narrow[:, h * rows : (h + 1) * rows]

    def pick(s, carry):
        sent[s] = low[jnp.maximum(tag[s], 0)]
        return carry

    lax.fori_loop(0, sent.shape[0], pick, 0, unroll=4)


def finish_kernel(extent_y, slot, scaled_in, blocks_in, received, out, scaled, blocks, picks, sems, pick_sems):
    panels = scaled.shape[0]
    per_leaf = slot.shape[0] // panels
    loads = []
    for g in range(panels // extent_y):
        part = pl.ds(g * extent_y, extent_y)
        load = [
            pltpu.make_async_copy(blocks_in.at[part], blocks.at[part], sems.at[2 * g]),
            pltpu.make_async_copy(scaled_in.at[part], scaled.at[part], sems.at[2 * g + 1]),
        ]
        for e in range(g * extent_y * per_leaf, (g + 1) * extent_y * per_leaf):
            load.append(pltpu.make_async_copy(received.at[slot[e]], picks.at[e], pick_sems.at[e]))
        for copy in load:
            copy.start()
        loads.append(load)
    for p in range(panels):
        x, y = divmod(p, extent_y)
        if y == 0:
            for copy in loads[x]:
                copy.wait()
        picked = [picks[p * per_leaf + k] for k in range(per_leaf)]
        acc = scaled[p] - dot(jnp.concatenate(picked, axis=1), blocks[p], "nn")
        out[:, x, y, :] = acc


def call(kernel, out_shape, in_specs, out_specs, limit, scratch=(), flops=0, moved=0):
    return pl.pallas_call(
        kernel,
        out_shape=out_shape,
        in_specs=in_specs,
        out_specs=out_specs,
        scratch_shapes=list(scratch),
        compiler_params=pltpu.CompilerParams(vmem_limit_bytes=limit * MIB),
        cost_estimate=pl.CostEstimate(flops=flops, bytes_accessed=moved, transcendentals=0),
    )


def level(
    voltage,
    source,
    conduct,
    leaf_inverse,
    update_rows,
    update_matrix,
    chain_slot,
    separator_source,
    separator_inverse,
    separator_coupling,
):
    fields, extent_x, extent_y, width = voltage.shape
    per_leaf = update_rows.shape[3]
    rows = update_matrix.shape[2] // per_leaf
    halves = width // rows
    panels = extent_x * extent_y
    chains = chain_slot.shape[0]
    sep_rows = separator_source.shape[1]
    owners = lax.axis_size("leaf")
    columns = lax.axis_size("col")
    entries = panels * per_leaf
    capacity = 2
    slots = owners * capacity
    shape = jax.ShapeDtypeStruct

    def shifted(block, axis, distance, wrap=False):
        size = lax.axis_size(axis)
        route = [(i, (i + distance) % size) for i in range(size) if wrap or 0 <= i + distance < size]
        return lax.ppermute(block, axis, route)

    fresh = lax.optimization_barrier(voltage)
    padded = call(
        pack_kernel,
        shape((sep_rows, 2 * width + 8 + panels, width), F32),
        [VM] * 4,
        VM,
        8,
        moved=2 << 20,
    )(
        separator_coupling,
        separator_inverse,
        jnp.transpose(fresh[:, :, :, width - 1].reshape(fields, panels)),
        jnp.transpose(fresh[:, :, :, 0].reshape(fields, panels)),
    )
    edges = (
        jnp.transpose(fresh[:, extent_x - 1], (1, 0, 2)),
        jnp.transpose(fresh[:, 0], (1, 0, 2)),
        padded.astype(jnp.float16),
    )
    last_x, first_x, packed = lax.optimization_barrier(edges)
    below = shifted(last_x, "leaf", 1)
    above = shifted(first_x, "leaf", -1)

    targets = update_rows.reshape(entries)
    chain_hit = (targets // halves)[:, None] == jnp.arange(chains, dtype=jnp.int32)
    target_slot = jnp.sum(jnp.where(chain_hit, chain_slot, 0), axis=1)
    owner = target_slot // sep_rows
    local = target_slot % sep_rows * halves + targets % halves
    ids = jnp.arange(entries, dtype=jnp.int32)
    same = (owner[:, None] == owner[None, :]) & (ids[None, :] < ids[:, None])
    slot = owner * capacity + jnp.sum(same.astype(jnp.int32), axis=1)
    slot_hit = slot[:, None] == jnp.arange(slots, dtype=jnp.int32)[None, :]
    out_tags = jnp.sum(jnp.where(slot_hit, local[:, None] + 1, 0), axis=0) - 1
    marks = jnp.pad(out_tags.astype(BF16).reshape(owners, capacity, 1), ((0, 0), (0, 8 - capacity), (0, 0)))
    marks = jnp.broadcast_to(marks, (owners, 8, rows))

    pieces = [padded] + [None] * (columns - 1)
    up = down = packed
    for hop in range(1, columns // 2):
        up = shifted(up, "col", 1, True)
        down = shifted(down, "col", -1, True)
        pieces[columns - hop] = up
        pieces[hop] = down
    column = lax.axis_index("col")
    left = pieces[columns - 1][0, 2 * width + 8 :, :fields].astype(F32)
    left = jnp.where(column > 0, left, 0.0)
    right = pieces[1][0, 2 * width + 8 :, fields : 2 * fields].astype(F32)
    right = jnp.where(column < columns - 1, right, 0.0)
    middle = sep_rows // 2
    up = shifted(up[:middle], "col", 1, True)
    down = shifted(down[middle:], "col", -1, True)
    for k in range(1, columns):
        if k != columns // 2:
            pieces[k] = pieces[k].astype(F32)
    pieces[columns // 2] = jnp.concatenate([up.astype(F32), down.astype(F32)], axis=0)

    blocks = update_matrix.reshape(panels, per_leaf * rows, width)
    inverse = leaf_inverse.reshape(panels, width, width)
    p_major = (1, 0, 2)
    low, sent = call(
        functools.partial(leaf_kernel, extent_y),
        (shape((panels, fields, width), BF16), shape((owners, capacity * fields + 8, rows), BF16)),
        [SM] + [VM] * 9,
        (VM, VM),
        12,
        flops=2 * panels * fields * width * width,
        moved=8 << 20,
    )(
        slot,
        jnp.transpose(voltage.reshape(fields, panels, width), p_major),
        jnp.transpose(source.reshape(fields, panels, width), p_major),
        (6.0 + conduct).reshape(panels, width),
        below,
        above,
        left,
        right,
        blocks,
        marks,
    )

    scaled = call(
        scaled_kernel,
        shape((panels, fields, width), F32),
        [VM, VM],
        VM,
        8,
        flops=2 * panels * fields * width * width,
        moved=6 << 20,
    )(low, inverse)

    def exchange(block):
        return lax.all_to_all(block, "leaf", split_axis=0, concat_axis=0, tiled=True)

    arrived = exchange(sent)
    drive, tags = call(
        functools.partial(owner_kernel, capacity),
        (shape((sep_rows, fields, width), BF16), shape((owners, rows), F32)),
        [VM, VM],
        (VM, VM),
        6,
        flops=slots * fields * rows,
        moved=3 << 20,
    )(arrived, jnp.transpose(separator_source, p_major))
    in_tags = tags[:, :capacity].reshape(slots).astype(jnp.int32)

    place = column.astype(jnp.int32).reshape(1)
    square = shape((columns, sep_rows, width, width), BF16)
    m_high, m_low = call(
        functools.partial(factor_kernel, columns),
        (square, square),
        [SM] + [HB] * columns,
        (VM, VM),
        FACTOR_MIB,
        scratch=[
            pltpu.VMEM((columns,) + packed.shape, F32),
            pltpu.VMEM((columns, sep_rows, width, width), F32),
            pltpu.VMEM((sep_rows, width, width), F32),
            pltpu.SemaphoreType.DMA((columns,)),
        ],
        flops=2 * 126 * width**3,
        moved=12 << 20,
    )(place, *pieces)

    drives = [drive] * columns
    for k in sorted(range(1, columns), key=lambda k: -min(k, columns - k)):
        drives[k] = shifted(drive, "col", -k, True)
    result, answer = call(
        functools.partial(solve_kernel, columns),
        (shape((sep_rows, fields, width), F32), shape((slots, fields, rows), BF16)),
        [SM] + [VM] * (2 + columns),
        (VM, VM),
        10,
        scratch=[pltpu.VMEM((sep_rows * halves, fields, rows), BF16)],
        flops=4 * columns * sep_rows * fields * width * width,
        moved=8 << 20,
    )(in_tags, m_high, m_low, *drives)
    returned = exchange(answer.reshape(owners, capacity, fields, rows)).reshape(slots, fields, rows)
    leaf_result = call(
        functools.partial(finish_kernel, extent_y),
        shape(voltage.shape, F32),
        [SM] + [HB] * 3,
        VM,
        56,
        scratch=[
            pltpu.VMEM((panels, fields, width), F32),
            pltpu.VMEM((panels, per_leaf * rows, width), BF16),
            pltpu.VMEM((entries, fields, rows), BF16),
            pltpu.SemaphoreType.DMA((2 * extent_x,)),
            pltpu.SemaphoreType.DMA((entries,)),
        ],
        flops=2 * panels * fields * width * width,
        moved=8 << 20,
    )(slot, scaled, blocks, returned)
    return leaf_result, jnp.transpose(result, p_major)


def solution(mesh):
    placed = (
        P(None, "leaf", None, "col"),
        P(None, "leaf", None, "col"),
        P("leaf", None, "col"),
        P("leaf", None, "col", None),
        P("col", "leaf", None, None),
        P("leaf", None, None, "col"),
        P(),
        P(None, "leaf", "col"),
        P("leaf", "col", None),
        P("leaf", "col", None),
    )
    return jax.shard_map(
        level,
        mesh=mesh,
        in_specs=placed,
        out_specs=(P(None, "leaf", None, "col"), P(None, "leaf", "col")),
        check_vma=False,
    )
```

```python
import functools
import jax
import jax.numpy as jnp
from jax import lax
from jax.experimental import pallas as pl
from jax.experimental.pallas import tpu as pltpu
from jax.sharding import PartitionSpec as P

VM = pl.BlockSpec(memory_space=pltpu.VMEM)
HB = pl.BlockSpec(memory_space=pltpu.HBM)
SM = pl.BlockSpec(memory_space=pltpu.SMEM)
F32 = jnp.float32
BF16 = jnp.bfloat16
MIB = 1 << 20
FACTOR_MIB = 56
SOLVE_MIB = 56


def dot(a, b, kind):
    dims = {"nt": (((1,), (1,)), ((), ())), "nn": (((1,), (0,)), ((), ()))}[kind]
    return lax.dot_general(a, b, dims, preferred_element_type=F32)


def split(x):
    high = x.astype(BF16)
    return high, (x - high.astype(F32)).astype(BF16)


def dot3(a, b, kind):
    high, low = split(a)
    b_high, b_low = split(b)
    axis = 1 if kind == "nt" else 0
    left = jnp.concatenate([high, low, high], axis=1)
    right = jnp.concatenate([b_high, b_high, b_low], axis=axis)
    return dot(left, right, kind)


def leaf_kernel(extent_y, slot, volt, source, diag, below, above, edge, blocks, marks, low_out, sent):
    panels, fields, width = volt.shape
    rows = sent.shape[2]
    per_leaf = slot.shape[0] // panels
    capacity = sent.shape[1] // fields
    sent[:, : capacity * fields, :] = jnp.zeros((sent.shape[0], capacity * fields, rows), BF16)
    sent[:, capacity * fields :, :] = marks[...]
    lane = lax.broadcasted_iota(jnp.int32, (fields, width), 1)
    rest = jnp.zeros((fields - 2 * panels, edge.shape[1]), F32)
    sides = jnp.transpose(jnp.concatenate([edge[...], rest], axis=0))
    for p in range(panels):
        y = p % extent_y
        center = volt[p].astype(F32)
        x_low = below[y] if p < extent_y else volt[p - extent_y]
        x_high = above[y] if p >= panels - extent_y else volt[p + extent_y]
        beside = x_high.astype(F32) + x_low.astype(F32)
        z_low = jnp.where(lane == 0, sides[:, p : p + 1], pltpu.roll(center, 1, 1))
        z_high = jnp.where(lane == width - 1, sides[:, panels + p : panels + p + 1], pltpu.roll(center, width - 1, 1))
        beside = beside + z_high + z_low
        if y + 1 < extent_y:
            beside = beside + volt[p + 1].astype(F32)
        if y > 0:
            beside = beside + volt[p - 1].astype(F32)
        residual = source[p].astype(F32) - (diag[p : p + 1, :] * center - beside)
        low = residual.astype(BF16)
        low_out[p] = low
        product = dot(low, blocks[p], "nt").astype(BF16)
        for k in range(per_leaf):
            s = slot[p * per_leaf + k]
            start = pl.multiple_of(lax.rem(s, capacity) * fields, fields)
            sent[lax.div(s, capacity), pl.ds(start, fields), :] = product[:, k * rows : (k + 1) * rows]


def scaled_kernel(low, inverse, out):
    for p in range(low.shape[0]):
        out[p] = dot(low[p], inverse[p], "nt")


def owner_kernel(capacity, received, own, drive, tags):
    sep_rows, fields, width = own.shape
    owners, _, rows = received.shape
    halves = width // rows
    count = sep_rows * halves
    step = 32

    def mark(s, r):
        return received[s, capacity * fields : capacity * fields + 8, :].astype(F32)[r : r + 1]

    lane = lax.broadcasted_iota(jnp.int32, (1, rows), 1)
    for s in range(owners):
        line = mark(s, 0)
        for r in range(1, capacity):
            line = jnp.where(lane == r, mark(s, r), line)
        tags[s : s + 1, :] = line
    for c in range(fields // step):
        span = slice(c * step, (c + 1) * step)
        first = []
        for b in range(count):
            first.append(own[b // halves, span, (b % halves) * rows : (b % halves + 1) * rows])

        def add(s, totals):
            totals = list(totals)
            for r in range(capacity):
                tag = jnp.broadcast_to(mark(s, r), (step, rows))
                start = r * fields + c * step
                block = received[s, start : start + step, :].astype(F32)
                for b in range(count):
                    totals[b] = totals[b] - jnp.where(tag == float(b), block, 0.0)
            return tuple(totals)

        totals = lax.fori_loop(0, owners, add, tuple(first), unroll=4)
        for b in range(count):
            drive[b // halves, span, (b % halves) * rows : (b % halves + 1) * rows] = totals[b].astype(BF16)


def pack_kernel(coupling, inverse, last_z, first_z, out):
    width = coupling.shape[2]
    for e in range(coupling.shape[0]):
        block = inverse[e]
        biggest = jnp.max(jnp.max(jnp.abs(block), axis=1, keepdims=True), axis=0, keepdims=True)
        power = jnp.clip(jnp.ceil(jnp.log2(biggest)), -120.0, 120.0)
        out[e, :width, :] = coupling[e]
        out[e, width : 2 * width, :] = block * jnp.exp2(-power)
        out[e, 2 * width : 2 * width + 8, :] = jnp.broadcast_to(power, (8, width))
        out[e, 2 * width + 8 :, :] = jnp.concatenate([last_z[...], first_z[...]], axis=1).astype(F32)


def factor_kernel(columns, place, *refs):
    pieces, (m_high, m_low, ring, z, y, sems) = refs[:columns], refs[columns:]
    chains, _, width = pieces[0].shape
    copies = [pltpu.make_async_copy(pieces[k], ring.at[k], sems.at[k]) for k in range(columns)]
    for copy in copies:
        copy.start()
    q = place[0]

    def at(p):
        return lax.rem(p - q + columns, columns)

    def coupling(rel, e):
        return ring[rel, e, :width, :]

    def inverse(rel, e):
        return ring[rel, e, width : 2 * width, :] * jnp.exp2(ring[rel, e, 2 * width : 2 * width + 1, :])

    row = lax.broadcasted_iota(jnp.int32, (width, width), 0)
    col = lax.broadcasted_iota(jnp.int32, (width, width), 1)
    eye = (row == col).astype(F32)
    copies[0].wait()
    for e in range(chains):
        z[q, e] = inverse(0, e)
        y[e] = eye
    for k in range(1, columns):
        copies[k].wait()

        @pl.when(q + k < columns)
        def _(k=k):
            out = [-dot3(y[e], coupling(k, e), "nt") for e in range(chains)]
            for e in range(chains):
                y[e] = out[e]
                z[q + k, e] = dot3(out[e], inverse(k, e), "nn")

    def put(p, xs):
        rel = at(p)
        for e in range(chains):
            high, low = split(xs[e])
            m_high[rel, e] = high
            m_low[rel, e] = low

    last = tuple(z[columns - 1, e] for e in range(chains))
    put(columns - 1, last)

    def up(i, xs):
        p = columns - 2 - i
        rel = at(p + 1)
        out = []
        for e in range(chains):
            x = -dot3(xs[e], coupling(rel, e), "nn")
            out.append(x + jnp.where(p >= q, z[p, e], 0.0))
        put(p, out)
        return tuple(out)

    lax.fori_loop(0, columns - 1, up, last)


def solve_kernel(columns, tag, m_high_in, m_low_in, *refs):
    drives, (result, sent, m_high, m_low, low, sems) = refs[:columns], refs[columns:]
    sep_rows, _, width = result.shape
    rows = sent.shape[2]
    halves = width // rows
    loads = []
    for k in range(columns):
        one = pltpu.make_async_copy(m_high_in.at[k], m_high.at[k], sems.at[2 * k])
        two = pltpu.make_async_copy(m_low_in.at[k], m_low.at[k], sems.at[2 * k + 1])
        one.start()
        two.start()
        loads.append((one, two))
    for k in range(columns):
        for load in loads[k]:
            load.wait()
        for e in range(sep_rows):
            d = drives[k][e]
            term = dot(d, m_high[k, e], "nt") + dot(d, m_low[k, e], "nt")
            result[e] = term if k == 0 else result[e] + term
    for e in range(sep_rows):
        narrow = result[e].astype(BF16)
        for h in range(halves):
            low[e * halves + h] = narrow[:, h * rows : (h + 1) * rows]

    def pick(s, carry):
        sent[s] = low[jnp.maximum(tag[s], 0)]
        return carry

    lax.fori_loop(0, sent.shape[0], pick, 0, unroll=4)


def finish_kernel(extent_y, slot, scaled_in, blocks_in, received, out, scaled, blocks, picks, sems, pick_sems):
    panels = scaled.shape[0]
    per_leaf = slot.shape[0] // panels
    loads = []
    for g in range(panels // extent_y):
        part = pl.ds(g * extent_y, extent_y)
        load = [
            pltpu.make_async_copy(blocks_in.at[part], blocks.at[part], sems.at[2 * g]),
            pltpu.make_async_copy(scaled_in.at[part], scaled.at[part], sems.at[2 * g + 1]),
        ]
        for e in range(g * extent_y * per_leaf, (g + 1) * extent_y * per_leaf):
            load.append(pltpu.make_async_copy(received.at[slot[e]], picks.at[e], pick_sems.at[e]))
        for copy in load:
            copy.start()
        loads.append(load)
    for p in range(panels):
        x, y = divmod(p, extent_y)
        if y == 0:
            for copy in loads[x]:
                copy.wait()
        picked = [picks[p * per_leaf + k] for k in range(per_leaf)]
        acc = scaled[p] - dot(jnp.concatenate(picked, axis=1), blocks[p], "nn")
        out[:, x, y, :] = acc


def call(kernel, out_shape, in_specs, out_specs, limit, scratch=(), flops=0, moved=0):
    return pl.pallas_call(
        kernel,
        out_shape=out_shape,
        in_specs=in_specs,
        out_specs=out_specs,
        scratch_shapes=list(scratch),
        compiler_params=pltpu.CompilerParams(vmem_limit_bytes=limit * MIB),
        cost_estimate=pl.CostEstimate(flops=flops, bytes_accessed=moved, transcendentals=0),
    )


def level(
    voltage,
    source,
    conduct,
    leaf_inverse,
    update_rows,
    update_matrix,
    chain_slot,
    separator_source,
    separator_inverse,
    separator_coupling,
):
    fields, extent_x, extent_y, width = voltage.shape
    per_leaf = update_rows.shape[3]
    rows = update_matrix.shape[2] // per_leaf
    halves = width // rows
    panels = extent_x * extent_y
    chains = chain_slot.shape[0]
    sep_rows = separator_source.shape[1]
    owners = lax.axis_size("leaf")
    columns = lax.axis_size("col")
    entries = panels * per_leaf
    capacity = 2
    slots = owners * capacity
    shape = jax.ShapeDtypeStruct

    def shifted(block, axis, distance, wrap=False):
        size = lax.axis_size(axis)
        route = [(i, (i + distance) % size) for i in range(size) if wrap or 0 <= i + distance < size]
        return lax.ppermute(block, axis, route)

    fresh = lax.optimization_barrier(voltage)
    padded = call(
        pack_kernel,
        shape((sep_rows, 2 * width + 8 + panels, width), F32),
        [VM] * 4,
        VM,
        8,
        moved=2 << 20,
    )(
        separator_coupling,
        separator_inverse,
        jnp.transpose(fresh[:, :, :, width - 1].reshape(fields, panels)),
        jnp.transpose(fresh[:, :, :, 0].reshape(fields, panels)),
    )
    edges = (
        jnp.transpose(fresh[:, extent_x - 1], (1, 0, 2)),
        jnp.transpose(fresh[:, 0], (1, 0, 2)),
        padded.astype(jnp.float16),
    )
    last_x, first_x, packed = lax.optimization_barrier(edges)
    below = shifted(last_x, "leaf", 1)
    above = shifted(first_x, "leaf", -1)

    targets = update_rows.reshape(entries)
    chain_hit = (targets // halves)[:, None] == jnp.arange(chains, dtype=jnp.int32)
    target_slot = jnp.sum(jnp.where(chain_hit, chain_slot, 0), axis=1)
    owner = target_slot // sep_rows
    local = target_slot % sep_rows * halves + targets % halves
    ids = jnp.arange(entries, dtype=jnp.int32)
    same = (owner[:, None] == owner[None, :]) & (ids[None, :] < ids[:, None])
    slot = owner * capacity + jnp.sum(same.astype(jnp.int32), axis=1)
    slot_hit = slot[:, None] == jnp.arange(slots, dtype=jnp.int32)[None, :]
    out_tags = jnp.sum(jnp.where(slot_hit, local[:, None] + 1, 0), axis=0) - 1
    marks = jnp.pad(out_tags.astype(BF16).reshape(owners, capacity, 1), ((0, 0), (0, 8 - capacity), (0, 0)))
    marks = jnp.broadcast_to(marks, (owners, 8, rows))

    pieces = [padded] + [None] * (columns - 1)
    up = down = packed
    for hop in range(1, columns // 2):
        up = shifted(up, "col", 1, True)
        down = shifted(down, "col", -1, True)
        pieces[columns - hop] = up
        pieces[hop] = down
    column = lax.axis_index("col")
    far = 2 * width + 8
    ids = jnp.arange(2 * panels, dtype=jnp.int32)[:, None]
    inside = jnp.where(ids < panels, column > 0, column < columns - 1)
    edge = jnp.concatenate([pieces[columns - 1][0, far:, :fields], pieces[1][0, far:, fields : 2 * fields]], axis=0)
    edge = jnp.where(inside, edge.astype(F32), 0.0)
    middle = sep_rows // 2
    up = shifted(up[:middle], "col", 1, True)
    down = shifted(down[middle:], "col", -1, True)
    for k in range(1, columns):
        if k != columns // 2:
            pieces[k] = pieces[k].astype(F32)
    pieces[columns // 2] = jnp.concatenate([up.astype(F32), down.astype(F32)], axis=0)

    blocks = update_matrix.reshape(panels, per_leaf * rows, width)
    inverse = leaf_inverse.reshape(panels, width, width)
    p_major = (1, 0, 2)
    low, sent = call(
        functools.partial(leaf_kernel, extent_y),
        (shape((panels, fields, width), BF16), shape((owners, capacity * fields + 8, rows), BF16)),
        [SM] + [VM] * 8,
        (VM, VM),
        12,
        flops=2 * panels * fields * width * width,
        moved=8 << 20,
    )(
        slot,
        jnp.transpose(voltage.reshape(fields, panels, width), p_major),
        jnp.transpose(source.reshape(fields, panels, width), p_major),
        (6.0 + conduct).reshape(panels, width),
        below,
        above,
        edge,
        blocks,
        marks,
    )

    scaled = call(
        scaled_kernel,
        shape((panels, fields, width), F32),
        [VM, VM],
        VM,
        8,
        flops=2 * panels * fields * width * width,
        moved=6 << 20,
    )(low, inverse)

    def exchange(block):
        return lax.all_to_all(block, "leaf", split_axis=0, concat_axis=0, tiled=True)

    arrived = exchange(sent)
    drive, tags = call(
        functools.partial(owner_kernel, capacity),
        (shape((sep_rows, fields, width), BF16), shape((owners, rows), F32)),
        [VM, VM],
        (VM, VM),
        6,
        flops=slots * fields * rows,
        moved=3 << 20,
    )(arrived, jnp.transpose(separator_source, p_major))
    in_tags = tags[:, :capacity].reshape(slots).astype(jnp.int32)

    place = column.astype(jnp.int32).reshape(1)
    square = shape((columns, sep_rows, width, width), BF16)
    m_high, m_low = call(
        functools.partial(factor_kernel, columns),
        (square, square),
        [SM] + [HB] * columns,
        (VM, VM),
        FACTOR_MIB,
        scratch=[
            pltpu.VMEM((columns,) + packed.shape, F32),
            pltpu.VMEM((columns, sep_rows, width, width), F32),
            pltpu.VMEM((sep_rows, width, width), F32),
            pltpu.SemaphoreType.DMA((columns,)),
        ],
        flops=2 * 126 * width**3,
        moved=12 << 20,
    )(place, *pieces)

    drives = [drive] * columns
    for k in (1, 2):
        drives[k] = shifted(drive, "col", -k, True)
        drives[columns - k] = shifted(drive, "col", k, True)
    ahead, behind = drives[2], drives[columns - 2]
    drives[3] = shifted(ahead, "col", -1, True)
    drives[columns - 3] = shifted(behind, "col", 1, True)
    low_part = shifted(ahead[:middle], "col", -2, True)
    high_part = shifted(behind[middle:], "col", 2, True)
    drives[4] = jnp.concatenate([low_part, high_part], axis=0)
    result, answer = call(
        functools.partial(solve_kernel, columns),
        (shape((sep_rows, fields, width), F32), shape((slots, fields, rows), BF16)),
        [SM] + [HB] * 2 + [VM] * columns,
        (VM, VM),
        SOLVE_MIB,
        scratch=[
            pltpu.VMEM(square.shape, BF16),
            pltpu.VMEM(square.shape, BF16),
            pltpu.VMEM((sep_rows * halves, fields, rows), BF16),
            pltpu.SemaphoreType.DMA((2 * columns,)),
        ],
        flops=4 * columns * sep_rows * fields * width * width,
        moved=8 << 20,
    )(in_tags, m_high, m_low, *drives)
    returned = exchange(answer.reshape(owners, capacity, fields, rows)).reshape(slots, fields, rows)
    leaf_result = call(
        functools.partial(finish_kernel, extent_y),
        shape(voltage.shape, F32),
        [SM] + [HB] * 3,
        VM,
        56,
        scratch=[
            pltpu.VMEM((panels, fields, width), F32),
            pltpu.VMEM((panels, per_leaf * rows, width), BF16),
            pltpu.VMEM((entries, fields, rows), BF16),
            pltpu.SemaphoreType.DMA((2 * extent_x,)),
            pltpu.SemaphoreType.DMA((entries,)),
        ],
        flops=2 * panels * fields * width * width,
        moved=8 << 20,
    )(slot, scaled, blocks, returned)
    return leaf_result, jnp.transpose(result, p_major)


def solution(mesh):
    placed = (
        P(None, "leaf", None, "col"),
        P(None, "leaf", None, "col"),
        P("leaf", None, "col"),
        P("leaf", None, "col", None),
        P("col", "leaf", None, None),
        P("leaf", None, None, "col"),
        P(),
        P(None, "leaf", "col"),
        P("leaf", "col", None),
        P("leaf", "col", None),
    )
    return jax.shard_map(
        level,
        mesh=mesh,
        in_specs=placed,
        out_specs=(P(None, "leaf", None, "col"), P(None, "leaf", "col")),
        check_vma=False,
    )
```

```python
import functools
import jax
import jax.numpy as jnp
from jax import lax
from jax.experimental import pallas as pl
from jax.experimental.pallas import tpu as pltpu
from jax.sharding import PartitionSpec as P

VM = pl.BlockSpec(memory_space=pltpu.VMEM)
HB = pl.BlockSpec(memory_space=pltpu.HBM)
SM = pl.BlockSpec(memory_space=pltpu.SMEM)
F32 = jnp.float32
BF16 = jnp.bfloat16
MIB = 1 << 20
FACTOR_MIB = 56
SOLVE_MIB = 56


def dot(a, b, kind):
    dims = {"nt": (((1,), (1,)), ((), ())), "nn": (((1,), (0,)), ((), ()))}[kind]
    return lax.dot_general(a, b, dims, preferred_element_type=F32)


def split(x):
    high = x.astype(BF16)
    return high, (x - high.astype(F32)).astype(BF16)


def dot3(a, b, kind):
    high, low = split(a)
    b_high, b_low = split(b)
    axis = 1 if kind == "nt" else 0
    left = jnp.concatenate([high, low, high], axis=1)
    right = jnp.concatenate([b_high, b_high, b_low], axis=axis)
    return dot(left, right, kind)


def leaf_kernel(extent_y, slot, volt, source, diag, below, above, edge, blocks, marks, low_out, sent):
    panels, fields, width = volt.shape
    rows = sent.shape[2]
    per_leaf = slot.shape[0] // panels
    capacity = sent.shape[1] // fields
    sent[:, : capacity * fields, :] = jnp.zeros((sent.shape[0], capacity * fields, rows), BF16)
    sent[:, capacity * fields :, :] = marks[...]
    lane = lax.broadcasted_iota(jnp.int32, (fields, width), 1)
    rest = jnp.zeros((fields - 2 * panels, edge.shape[1]), F32)
    sides = jnp.transpose(jnp.concatenate([edge[...], rest], axis=0))
    for p in range(panels):
        y = p % extent_y
        center = volt[p].astype(F32)
        x_low = below[y] if p < extent_y else volt[p - extent_y]
        x_high = above[y] if p >= panels - extent_y else volt[p + extent_y]
        beside = x_high.astype(F32) + x_low.astype(F32)
        z_low = jnp.where(lane == 0, sides[:, p : p + 1], pltpu.roll(center, 1, 1))
        z_high = jnp.where(lane == width - 1, sides[:, panels + p : panels + p + 1], pltpu.roll(center, width - 1, 1))
        beside = beside + z_high + z_low
        if y + 1 < extent_y:
            beside = beside + volt[p + 1].astype(F32)
        if y > 0:
            beside = beside + volt[p - 1].astype(F32)
        residual = source[p].astype(F32) - (diag[p : p + 1, :] * center - beside)
        low = residual.astype(BF16)
        low_out[p] = low
        product = dot(low, blocks[p], "nt").astype(BF16)
        for k in range(per_leaf):
            s = slot[p * per_leaf + k]
            start = pl.multiple_of(lax.rem(s, capacity) * fields, fields)
            sent[lax.div(s, capacity), pl.ds(start, fields), :] = product[:, k * rows : (k + 1) * rows]


def scaled_kernel(low, inverse, out):
    for p in range(low.shape[0]):
        out[p] = dot(low[p], inverse[p], "nt")


def owner_kernel(capacity, received, own, drive, tags):
    sep_rows, fields, width = own.shape
    owners, _, rows = received.shape
    halves = width // rows
    count = sep_rows * halves
    step = 32

    def mark(s, r):
        return received[s, capacity * fields : capacity * fields + 8, :].astype(F32)[r : r + 1]

    lane = lax.broadcasted_iota(jnp.int32, (1, rows), 1)
    for s in range(owners):
        line = mark(s, 0)
        for r in range(1, capacity):
            line = jnp.where(lane == r, mark(s, r), line)
        tags[s : s + 1, :] = line
    for c in range(fields // step):
        span = slice(c * step, (c + 1) * step)
        first = []
        for b in range(count):
            first.append(own[b // halves, span, (b % halves) * rows : (b % halves + 1) * rows])

        def add(s, totals):
            totals = list(totals)
            for r in range(capacity):
                tag = jnp.broadcast_to(mark(s, r), (step, rows))
                start = r * fields + c * step
                block = received[s, start : start + step, :].astype(F32)
                for b in range(count):
                    totals[b] = totals[b] - jnp.where(tag == float(b), block, 0.0)
            return tuple(totals)

        totals = lax.fori_loop(0, owners, add, tuple(first), unroll=4)
        for b in range(count):
            drive[b // halves, span, (b % halves) * rows : (b % halves + 1) * rows] = totals[b].astype(BF16)


def pack_kernel(coupling, inverse, last_z, first_z, out):
    width = coupling.shape[2]
    for e in range(coupling.shape[0]):
        block = inverse[e]
        biggest = jnp.max(jnp.max(jnp.abs(block), axis=1, keepdims=True), axis=0, keepdims=True)
        power = jnp.clip(jnp.ceil(jnp.log2(biggest)), -120.0, 120.0)
        out[e, :width, :] = coupling[e]
        out[e, width : 2 * width, :] = block * jnp.exp2(-power)
        out[e, 2 * width : 2 * width + 8, :] = jnp.broadcast_to(power, (8, width))
        out[e, 2 * width + 8 :, :] = jnp.concatenate([last_z[...], first_z[...]], axis=1).astype(F32)


def factor_kernel(columns, place, *refs):
    pieces, (high_out, low_out, m_high, m_low, ring, z, y, sems, out_sems) = refs[:columns], refs[columns:]
    chains, _, width = pieces[0].shape
    copies = [pltpu.make_async_copy(pieces[k], ring.at[k], sems.at[k]) for k in range(columns)]
    for copy in copies:
        copy.start()
    q = place[0]

    def at(p):
        return lax.rem(p - q + columns, columns)

    def coupling(rel, e):
        return ring[rel, e, :width, :]

    def inverse(rel, e):
        return ring[rel, e, width : 2 * width, :] * jnp.exp2(ring[rel, e, 2 * width : 2 * width + 1, :])

    row = lax.broadcasted_iota(jnp.int32, (width, width), 0)
    col = lax.broadcasted_iota(jnp.int32, (width, width), 1)
    eye = (row == col).astype(F32)
    copies[0].wait()
    for e in range(chains):
        z[q, e] = inverse(0, e)
        y[e] = eye
    for k in range(1, columns):
        copies[k].wait()

        @pl.when(q + k < columns)
        def _(k=k):
            out = [-dot3(y[e], coupling(k, e), "nt") for e in range(chains)]
            for e in range(chains):
                y[e] = out[e]
                z[q + k, e] = dot3(out[e], inverse(k, e), "nn")

    def put(p, xs):
        rel = at(p)
        for e in range(chains):
            high, low = split(xs[e])
            m_high[rel, e] = high
            m_low[rel, e] = low
        pltpu.make_async_copy(m_high.at[rel], high_out.at[rel], out_sems.at[rel]).start()
        pltpu.make_async_copy(m_low.at[rel], low_out.at[rel], out_sems.at[columns + rel]).start()

    last = tuple(z[columns - 1, e] for e in range(chains))
    put(columns - 1, last)

    def up(i, xs):
        p = columns - 2 - i
        rel = at(p + 1)
        out = []
        for e in range(chains):
            x = -dot3(xs[e], coupling(rel, e), "nn")
            out.append(x + jnp.where(p >= q, z[p, e], 0.0))
        put(p, out)
        return tuple(out)

    lax.fori_loop(0, columns - 1, up, last)
    for k in range(columns):
        pltpu.make_async_copy(m_high.at[k], high_out.at[k], out_sems.at[k]).wait()
        pltpu.make_async_copy(m_low.at[k], low_out.at[k], out_sems.at[columns + k]).wait()


def solve_kernel(columns, tag, m_high_in, m_low_in, *refs):
    drives, (extra, result, sent, m_high, m_low, low, sems) = refs[:columns], refs[columns:]
    sep_rows, _, width = result.shape
    rows = sent.shape[2]
    halves = width // rows
    loads = []
    for k in range(columns):
        one = pltpu.make_async_copy(m_high_in.at[k], m_high.at[k], sems.at[2 * k])
        two = pltpu.make_async_copy(m_low_in.at[k], m_low.at[k], sems.at[2 * k + 1])
        one.start()
        two.start()
        loads.append((one, two))
    for k in range(columns):
        for load in loads[k]:
            load.wait()
        for e in range(sep_rows):
            half = drives[k].shape[0]
            d = drives[k][e] if e < half else extra[e - half]
            term = dot(d, m_high[k, e], "nt") + dot(d, m_low[k, e], "nt")
            result[e] = term if k == 0 else result[e] + term
    for e in range(sep_rows):
        narrow = result[e].astype(BF16)
        for h in range(halves):
            low[e * halves + h] = narrow[:, h * rows : (h + 1) * rows]

    def pick(s, carry):
        sent[s] = low[jnp.maximum(tag[s], 0)]
        return carry

    lax.fori_loop(0, sent.shape[0], pick, 0, unroll=4)


def finish_kernel(extent_y, slot, scaled_in, blocks_in, received, out, scaled, blocks, picks, sems, pick_sems):
    panels = scaled.shape[0]
    per_leaf = slot.shape[0] // panels
    loads = []
    for g in range(panels // extent_y):
        part = pl.ds(g * extent_y, extent_y)
        load = [
            pltpu.make_async_copy(blocks_in.at[part], blocks.at[part], sems.at[2 * g]),
            pltpu.make_async_copy(scaled_in.at[part], scaled.at[part], sems.at[2 * g + 1]),
        ]
        for e in range(g * extent_y * per_leaf, (g + 1) * extent_y * per_leaf):
            load.append(pltpu.make_async_copy(received.at[slot[e]], picks.at[e], pick_sems.at[e]))
        for copy in load:
            copy.start()
        loads.append(load)
    for p in range(panels):
        x, y = divmod(p, extent_y)
        if y == 0:
            for copy in loads[x]:
                copy.wait()
        picked = [picks[p * per_leaf + k] for k in range(per_leaf)]
        acc = scaled[p] - dot(jnp.concatenate(picked, axis=1), blocks[p], "nn")
        out[:, x, y, :] = acc


def call(kernel, out_shape, in_specs, out_specs, limit, scratch=(), flops=0, moved=0):
    return pl.pallas_call(
        kernel,
        out_shape=out_shape,
        in_specs=in_specs,
        out_specs=out_specs,
        scratch_shapes=list(scratch),
        compiler_params=pltpu.CompilerParams(vmem_limit_bytes=limit * MIB),
        cost_estimate=pl.CostEstimate(flops=flops, bytes_accessed=moved, transcendentals=0),
    )


def level(
    voltage,
    source,
    conduct,
    leaf_inverse,
    update_rows,
    update_matrix,
    chain_slot,
    separator_source,
    separator_inverse,
    separator_coupling,
):
    fields, extent_x, extent_y, width = voltage.shape
    per_leaf = update_rows.shape[3]
    rows = update_matrix.shape[2] // per_leaf
    halves = width // rows
    panels = extent_x * extent_y
    chains = chain_slot.shape[0]
    sep_rows = separator_source.shape[1]
    owners = lax.axis_size("leaf")
    columns = lax.axis_size("col")
    entries = panels * per_leaf
    capacity = 2
    slots = owners * capacity
    shape = jax.ShapeDtypeStruct

    def shifted(block, axis, distance, wrap=False):
        size = lax.axis_size(axis)
        route = [(i, (i + distance) % size) for i in range(size) if wrap or 0 <= i + distance < size]
        return lax.ppermute(block, axis, route)

    fresh = lax.optimization_barrier(voltage)
    padded = call(
        pack_kernel,
        shape((sep_rows, 2 * width + 8 + panels, width), F32),
        [VM] * 4,
        VM,
        8,
        moved=2 << 20,
    )(
        separator_coupling,
        separator_inverse,
        jnp.transpose(fresh[:, :, :, width - 1].reshape(fields, panels)),
        jnp.transpose(fresh[:, :, :, 0].reshape(fields, panels)),
    )
    edges = (
        jnp.transpose(fresh[:, extent_x - 1], (1, 0, 2)),
        jnp.transpose(fresh[:, 0], (1, 0, 2)),
        padded.astype(jnp.float16),
    )
    last_x, first_x, packed = lax.optimization_barrier(edges)
    below = shifted(last_x, "leaf", 1)
    above = shifted(first_x, "leaf", -1)

    targets = update_rows.reshape(entries)
    chain_hit = (targets // halves)[:, None] == jnp.arange(chains, dtype=jnp.int32)
    target_slot = jnp.sum(jnp.where(chain_hit, chain_slot, 0), axis=1)
    owner = target_slot // sep_rows
    local = target_slot % sep_rows * halves + targets % halves
    ids = jnp.arange(entries, dtype=jnp.int32)
    same = (owner[:, None] == owner[None, :]) & (ids[None, :] < ids[:, None])
    slot = owner * capacity + jnp.sum(same.astype(jnp.int32), axis=1)
    slot_hit = slot[:, None] == jnp.arange(slots, dtype=jnp.int32)[None, :]
    out_tags = jnp.sum(jnp.where(slot_hit, local[:, None] + 1, 0), axis=0) - 1
    marks = jnp.pad(out_tags.astype(BF16).reshape(owners, capacity, 1), ((0, 0), (0, 8 - capacity), (0, 0)))
    marks = jnp.broadcast_to(marks, (owners, 8, rows))

    pieces = [padded] + [None] * (columns - 1)
    up = down = packed
    for hop in range(1, columns // 2):
        up = shifted(up, "col", 1, True)
        down = shifted(down, "col", -1, True)
        pieces[columns - hop] = up
        pieces[hop] = down
    column = lax.axis_index("col")
    far = 2 * width + 8
    ids = jnp.arange(2 * panels, dtype=jnp.int32)[:, None]
    inside = jnp.where(ids < panels, column > 0, column < columns - 1)
    edge = jnp.concatenate([pieces[columns - 1][0, far:, :fields], pieces[1][0, far:, fields : 2 * fields]], axis=0)
    edge = jnp.where(inside, edge.astype(F32), 0.0)
    middle = sep_rows // 2
    up = shifted(up[:middle], "col", 1, True)
    down = shifted(down[middle:], "col", -1, True)
    for k in range(1, columns):
        if k != columns // 2:
            pieces[k] = pieces[k].astype(F32)
    pieces[columns // 2] = jnp.concatenate([up.astype(F32), down.astype(F32)], axis=0)

    blocks = update_matrix.reshape(panels, per_leaf * rows, width)
    inverse = leaf_inverse.reshape(panels, width, width)
    p_major = (1, 0, 2)
    low, sent = call(
        functools.partial(leaf_kernel, extent_y),
        (shape((panels, fields, width), BF16), shape((owners, capacity * fields + 8, rows), BF16)),
        [SM] + [VM] * 8,
        (VM, VM),
        12,
        flops=2 * panels * fields * width * width,
        moved=8 << 20,
    )(
        slot,
        jnp.transpose(voltage.reshape(fields, panels, width), p_major),
        jnp.transpose(source.reshape(fields, panels, width), p_major),
        (6.0 + conduct).reshape(panels, width),
        below,
        above,
        edge,
        blocks,
        marks,
    )

    scaled = call(
        scaled_kernel,
        shape((panels, fields, width), F32),
        [VM, VM],
        VM,
        8,
        flops=2 * panels * fields * width * width,
        moved=6 << 20,
    )(low, inverse)

    def exchange(block):
        return lax.all_to_all(block, "leaf", split_axis=0, concat_axis=0, tiled=True)

    arrived = exchange(sent)
    drive, tags = call(
        functools.partial(owner_kernel, capacity),
        (shape((sep_rows, fields, width), BF16), shape((owners, rows), F32)),
        [VM, VM],
        (VM, VM),
        6,
        flops=slots * fields * rows,
        moved=3 << 20,
    )(arrived, jnp.transpose(separator_source, p_major))
    in_tags = tags[:, :capacity].reshape(slots).astype(jnp.int32)

    place = column.astype(jnp.int32).reshape(1)
    square = shape((columns, sep_rows, width, width), BF16)
    m_high, m_low = call(
        functools.partial(factor_kernel, columns),
        (square, square),
        [SM] + [HB] * columns,
        (HB, HB),
        FACTOR_MIB,
        scratch=[
            pltpu.VMEM(square.shape, BF16),
            pltpu.VMEM(square.shape, BF16),
            pltpu.VMEM((columns,) + packed.shape, F32),
            pltpu.VMEM((columns, sep_rows, width, width), F32),
            pltpu.VMEM((sep_rows, width, width), F32),
            pltpu.SemaphoreType.DMA((columns,)),
            pltpu.SemaphoreType.DMA((2 * columns,)),
        ],
        flops=2 * 126 * width**3,
        moved=12 << 20,
    )(place, *pieces)

    drives = [drive] * columns
    for k in (1, 2):
        drives[k] = shifted(drive, "col", -k, True)
        drives[columns - k] = shifted(drive, "col", k, True)
    ahead, behind = drives[2], drives[columns - 2]
    drives[3] = shifted(ahead, "col", -1, True)
    drives[columns - 3] = shifted(behind, "col", 1, True)
    low_part = shifted(ahead[:middle], "col", -2, True)
    high_part = shifted(behind[middle:], "col", 2, True)
    drives[columns // 2] = low_part
    result, answer = call(
        functools.partial(solve_kernel, columns),
        (shape((sep_rows, fields, width), F32), shape((slots, fields, rows), BF16)),
        [SM] + [HB] * 2 + [VM] * (columns + 1),
        (VM, VM),
        SOLVE_MIB,
        scratch=[
            pltpu.VMEM(square.shape, BF16),
            pltpu.VMEM(square.shape, BF16),
            pltpu.VMEM((sep_rows * halves, fields, rows), BF16),
            pltpu.SemaphoreType.DMA((2 * columns,)),
        ],
        flops=4 * columns * sep_rows * fields * width * width,
        moved=8 << 20,
    )(in_tags, m_high, m_low, *drives, high_part)
    returned = exchange(answer.reshape(owners, capacity, fields, rows)).reshape(slots, fields, rows)
    leaf_result = call(
        functools.partial(finish_kernel, extent_y),
        shape(voltage.shape, F32),
        [SM] + [HB] * 3,
        VM,
        56,
        scratch=[
            pltpu.VMEM((panels, fields, width), F32),
            pltpu.VMEM((panels, per_leaf * rows, width), BF16),
            pltpu.VMEM((entries, fields, rows), BF16),
            pltpu.SemaphoreType.DMA((2 * extent_x,)),
            pltpu.SemaphoreType.DMA((entries,)),
        ],
        flops=2 * panels * fields * width * width,
        moved=8 << 20,
    )(slot, scaled, blocks, returned)
    return leaf_result, jnp.transpose(result, p_major)


def solution(mesh):
    placed = (
        P(None, "leaf", None, "col"),
        P(None, "leaf", None, "col"),
        P("leaf", None, "col"),
        P("leaf", None, "col", None),
        P("col", "leaf", None, None),
        P("leaf", None, None, "col"),
        P(),
        P(None, "leaf", "col"),
        P("leaf", "col", None),
        P("leaf", "col", None),
    )
    return jax.shard_map(
        level,
        mesh=mesh,
        in_specs=placed,
        out_specs=(P(None, "leaf", None, "col"), P(None, "leaf", "col")),
        check_vma=False,
    )
```
